32 devices in a mesh: beam: 2 (over y), fft: 4 (over z), chan: 4 (over x, core).
Axes of the slice: x: 2, y: 2, z: 4, core: 2. Of those that a mesh axis runs over, the one named last changes fastest.
Arguments:
- filterbank: bfloat16 [8192, 16384], P(('beam', 'chan'), 'fft'), parts along dimension 0, may hold values from -6 to 6
- delays: int32 [4096, 16], P('chan'), may hold values from 0 to 15, as said below
- template_bank: bfloat16 [2, 128, 32], replicated, may hold values from -1 to 1
- accel_index: int32 [64], replicated, may hold values from 0 to 127, as said below
Outputs:
- peaks: float32 [32, 64, 64], P(('beam', 'fft', 'chan')), parts along dimension 0
- energy: float32 [32], P(('beam', 'fft', 'chan')), parts along dimension 0
The draws below stay inside these ranges and needn't reach their ends.
There are 2 independent parts, one for each index of `beam`. The reference program is written for one: setup_inputs(seed, part) draws one part's arguments, and reference() takes and returns one part's arrays. A program takes and returns all parts, laid end to end along the dimension named above; an argument that names none is the same for every part. Nothing has to cross between parts.
Inputs may be any that keep to these rules, and one draw needn't show every extreme that they name: `delays`: follows the cold-plasma law: proportional to the trial measure times the channel's inverse squared frequency less that of the band's top, rounded down; the trial measures rise over the whole range; non-increasing along channels and non-decreasing along trial measures; the first channel reaches 15 at the last trial measure. `accel_index`: distinct and increasing; the first is 0 and the last is 127.
All inputs are finite; a program needn't handle non-finite values.
Results may differ from the reference program's by a relative error of at most 0.0021.
Values may be sent and summed in bfloat16 or wider, within the bound.
A program may use at most 64 MiB of HBM per device.

```python
import jax
import jax.numpy as jnp
from jax import lax

CHAN = 4096
MAXD = 16
WID = 32
NACC = 64
ZBANK = 128
NDM = 16
NSAMP = 16384


def draw_accel_index(key, part):
    interior = jax.random.permutation(jax.random.fold_in(key, 11), ZBANK - 2)[:NACC - 2] + 1
    chosen = jnp.concatenate([jnp.zeros((1,), jnp.int32), interior.astype(jnp.int32), jnp.full((1,), ZBANK - 1, jnp.int32)])
    return jnp.sort(chosen)


def draw_delays(key, part):
    steps_drawn = jax.random.randint(jax.random.fold_in(key, 23), (NDM,), 1, 3).astype(jnp.int32)
    rising = jnp.cumsum(steps_drawn).astype(jnp.int32) - steps_drawn[0]
    last_step = rising[NDM - 1]
    freqs = CHAN + jnp.arange(CHAN, dtype=jnp.int32)
    top_freq = 2 * CHAN
    scale_top = 2 ** 30 // (top_freq * top_freq)
    lags = 2 ** 30 // (freqs * freqs) - scale_top
    lags = lags.astype(jnp.int32)
    lowest = lags[0]
    numer = lags[:, None] * (MAXD - 1) * rising[None, :]
    table = numer // (lowest * last_step)
    return table.astype(jnp.int32)


def steps_of(rng, shape, cuts, low, top_value):
    def one(position, blocks):
        draws = jax.random.uniform(jax.random.fold_in(jax.random.fold_in(rng, 6), position), (blocks,), jnp.float32, low / len(cuts), top_value / len(cuts))
        return jnp.repeat(jnp.exp(draws), shape[position] // blocks).reshape((-1,) + (1,) * (len(shape) - position - 1))

    gain = one(*cuts[0])
    for cut in cuts[1:]:
        gain = gain * one(*cut)
    return gain


def gaussian(own_key, shape, scale, most, split=(), held_as=jnp.bfloat16):
    gain = steps_of(own_key, shape, split, -0.22, 0.18) if split else 1.0
    result = jax.random.normal(own_key, shape, jnp.float32) * scale * gain
    return jnp.minimum(jnp.maximum(result, -most), most).astype(held_as)


def setup_inputs(seed: int = 0, part: int = 0) -> dict:
    key_list = jax.random.split(jax.random.key(seed), 5)
    part_keys = jax.random.split(jax.random.fold_in(key_list[4], part), 5)
    filterbank = gaussian(part_keys[0], (CHAN, NSAMP), 1.0, 6.0, ((0, 4), (1, 4)))
    delays = draw_delays(jax.random.fold_in(key_list[4], 71), part)
    template_bank = gaussian(key_list[2], (2, ZBANK, WID), WID ** -0.5, 1.0)
    accel_index = draw_accel_index(jax.random.fold_in(key_list[4], 71), part)
    return {"filterbank": filterbank, "delays": delays, "template_bank": template_bank, "accel_index": accel_index}


def reference(filterbank, delays, template_bank, accel_index):
    channels, length = filterbank.shape
    block_count = length // 128
    padded = jnp.concatenate([filterbank, jnp.zeros((channels, MAXD * 128), filterbank.dtype)], axis=1)
    padded = padded.reshape(channels, block_count + MAXD, 128)
    starts = jnp.arange(block_count, dtype=jnp.int32)

    def one_measure(column):
        index_table = starts[None, :] + column.astype(jnp.int32)[:, None]
        picked = jnp.take_along_axis(padded, index_table[:, :, None], axis=1)
        return jnp.sum(picked.astype(jnp.float32), axis=0).reshape(length)

    series = lax.map(one_measure, delays.T) * (CHAN ** -0.5)
    bin_total = length // 2
    transform = jnp.fft.fft(series, axis=1)[:, :bin_total] * (length ** -0.5)
    spec_real = jnp.real(transform).astype(jnp.float32)
    spec_imag = jnp.imag(transform).astype(jnp.float32)
    round_real = spec_real.astype(jnp.bfloat16)
    round_imag = spec_imag.astype(jnp.bfloat16)
    kernel_stack = jnp.concatenate([template_bank[0][accel_index], template_bank[1][accel_index]], axis=0)
    templates = accel_index.shape[0]
    lead_taps = WID // 2

    def one_row(pair):
        row_real, row_imag = pair
        pad_real = jnp.pad(row_real, (lead_taps, WID - lead_taps))
        pad_imag = jnp.pad(row_imag, (lead_taps, WID - lead_taps))
        win_real = jnp.stack([pad_real[lag_index:lag_index + bin_total] for lag_index in range(WID)], axis=0)
        win_imag = jnp.stack([pad_imag[lag_index:lag_index + bin_total] for lag_index in range(WID)], axis=0)
        from_real = jnp.dot(kernel_stack, win_real, preferred_element_type=jnp.float32)
        from_imag = jnp.dot(kernel_stack, win_imag, preferred_element_type=jnp.float32)
        out_real = from_real[:templates] - from_imag[templates:]
        out_imag = from_imag[:templates] + from_real[templates:]
        power = out_real * out_real + out_imag * out_imag
        return jnp.max(power.reshape(templates, bin_total // 128, 128), axis=2)

    peaks = lax.map(one_row, (round_real, round_imag))
    energy = jnp.sum(spec_real * spec_real + spec_imag * spec_imag, axis=1)
    return (peaks, energy)
```

```python
import functools

import jax
import jax.numpy as jnp
import numpy as np
from jax import lax
from jax.experimental import pallas as pl
from jax.experimental.pallas import tpu as pltpu
from jax.sharding import PartitionSpec as P

MAXD = 16
LANES = 128
MESH = pl.DeviceIdType.MESH
HIGHEST = lax.Precision.HIGHEST


def tables(length, channels_total):
    wide = length // LANES
    half = wide // 2
    rows = np.arange(LANES)
    cols = np.arange(wide)
    outs = np.arange(half)
    first = 2 * np.pi * (rows[:, None] * rows[None, :] % LANES) / LANES
    one = np.concatenate([np.cos(first), -np.sin(first)], axis=0)
    turn = 2 * np.pi * (rows[:, None] * cols[None, :] % length) / length
    scale = channels_total ** -0.5 * length ** -0.5
    twist = np.stack([np.cos(turn), np.sin(turn)]) * scale
    second = 2 * np.pi * (cols[:, None] * outs[None, :] % wide) / wide
    c2, s2 = np.cos(second), np.sin(second)
    real = np.concatenate([c2, s2], axis=0)
    imag = np.concatenate([-s2, c2], axis=0)
    two = np.concatenate([real, real, imag, imag], axis=1)
    return [jnp.asarray(t, jnp.float32) for t in (one, twist, two)]


def kernel(
    sizes,
    fb_ref, delay_ref, bank_ref, accel_ref, one_ref, twist_ref, two_ref,
    peaks_ref, energy_ref,
    xbuf, picked, acc, part, r1, q, r2, total, r3, grid_ref, tmat,
    fsem, s1, v1, s2, v2, s3, v3,
):
    fft, xs, cores, dms, blocks, chunk = sizes
    chan = xs * cores
    span = blocks + MAXD
    f = lax.axis_index("fft")
    c = lax.axis_index("chan")
    x, core = c // cores, c % cores
    columns = fb_ref.shape[1]
    chunks = columns // chunk

    def fetch(i):
        start = pl.multiple_of(i * chunk, chunk)
        return pltpu.make_async_copy(
            fb_ref.at[:, pl.ds(start, chunk)], xbuf.at[i], fsem.at[i]
        )

    for i in range(chunks):
        fetch(i).start()

    barrier = pltpu.get_barrier_semaphore()
    for k in range(1, cores):
        pl.semaphore_signal(
            barrier, inc=1, device_id={"chan": x * cores + (core + k) % cores}, device_id_type=MESH
        )
    for k in range(1, xs):
        pl.semaphore_signal(
            barrier, inc=1, device_id={"chan": ((x + k) % xs) * cores + core}, device_id_type=MESH
        )
    for k in range(1, fft):
        pl.semaphore_signal(barrier, inc=1, device_id={"fft": (f + k) % fft}, device_id_type=MESH)

    lag = delay_ref[...]
    for o in range(MAXD):
        picked[(MAXD - 1 - o) * dms:(MAXD - o) * dms, :] = jnp.where(lag == o, 1.0, 0.0).astype(
            jnp.bfloat16
        )
    acc[...] = jnp.zeros_like(acc)

    def gather_columns(i, carry):
        fetch(i).wait()
        for b in range(chunk // 256):
            y = jnp.dot(
                picked[...], xbuf[i, :, b * 256:(b + 1) * 256], preferred_element_type=jnp.float32
            )
            for h in range(2):
                row = pl.multiple_of((i * (chunk // LANES) + 2 * b + h + 1) * dms, dms)
                acc[pl.ds(row, MAXD * dms), :] += y[:, h * LANES:(h + 1) * LANES]
        return carry

    lax.fori_loop(0, chunks, gather_columns, 0)

    for k in range(cores):
        for s in range(xs):
            for g in range(fft):
                d = g * chan + s * cores + k
                part[k, s, g] = acc[pl.ds(d, span, stride=dms), :]

    others = (cores - 1) + (xs - 1) + (fft - 1)
    pl.semaphore_wait(barrier, others)

    peer = (core + 1) % cores
    order = list(range(1, fft)) + [0]

    def to_core(s, k):
        xd, g = (x + s) % xs, (f + k) % fft
        return pltpu.make_async_remote_copy(
            part.at[peer, xd, g], r1.at[s, k], s1.at[s, k], v1.at[s, k],
            device_id={"chan": x * cores + peer}, device_id_type=MESH,
        )

    def to_x(s, k):
        return pltpu.make_async_remote_copy(
            q.at[s, k], r2.at[s, k], s2.at[s, k], v2.at[s, k],
            device_id={"chan": ((x + s) % xs) * cores + core}, device_id_type=MESH,
        )

    def to_fft(k):
        return pltpu.make_async_remote_copy(
            total.at[k], r3.at[k], s3.at[k], v3.at[k],
            device_id={"fft": (f + k) % fft}, device_id_type=MESH,
        )

    for k in order:
        for s in list(range(1, xs)) + [0]:
            to_core(s, k).start()
    for k in order:
        for s in range(1, xs):
            to_core(s, k).wait()
            q[s, k] = part[core, (x + s) % xs, (f + k) % fft] + r1[s, k]
            to_x(s, k).start()
    for k in order:
        to_core(0, k).wait()
        value = part[core, x, (f + k) % fft] + r1[0, k]
        for s in range(1, xs):
            to_x(s, k).wait()
            value = value + r2[s, k]
        total[k] = value
        if k:
            to_fft(k).start()

    accel = accel_ref[...]
    bank = bank_ref.shape[1]
    accels = accel.shape[1]
    taps = bank_ref.shape[2]
    chosen = jnp.where(
        lax.broadcasted_iota(jnp.int32, (bank, accels), 0) == accel, 1.0, 0.0
    ).astype(jnp.bfloat16)
    rows = []
    for part_index in range(2):
        row = lax.dot_general(
            chosen, bank_ref[part_index], (((0,), (0,)), ((), ())),
            preferred_element_type=jnp.float32,
        )
        rows.append(jnp.concatenate([row, jnp.zeros((accels, LANES - taps), jnp.float32)], axis=1))
    for kk in range(LANES // 2):
        for part_index in range(2):
            shifted = pltpu.roll(rows[part_index], kk, 1) if kk else rows[part_index]
            tmat[kk * accels:(kk + 1) * accels, part_index * LANES:(part_index + 1) * LANES] = (
                shifted.astype(jnp.bfloat16)
            )

    for k in range(1, fft):
        to_fft(k).wait()
    for z in range(fft):
        own = (f - z + fft) % fft
        def place(z=z, own=own):
            src = r3[own]
            grid_ref[z * blocks:(z + 1) * blocks, :] = src[MAXD:, :]
            if z:
                grid_ref[z * blocks - MAXD:z * blocks, :] += src[:MAXD, :]
        if z == 0:
            r3[0] = total[0]
        place()

    wide = grid_ref.shape[0]
    half = wide // 2
    data = grid_ref[...] if wide == LANES else grid_ref[...].reshape(LANES, wide)
    mixed = jnp.dot(one_ref[...], data, precision=HIGHEST, preferred_element_type=jnp.float32)
    re, im = mixed[:LANES], mixed[LANES:]
    tc, ts = twist_ref[0], twist_ref[1]
    turned = jnp.concatenate([re * tc + im * ts, im * tc - re * ts], axis=1)
    spec = jnp.dot(turned, two_ref[...], precision=HIGHEST, preferred_element_type=jnp.float32)

    lane = lax.broadcasted_iota(jnp.int32, (16, 2 * half), 1)
    low = lax.broadcasted_iota(jnp.int32, (64, 2 * half), 1) < half
    low16 = lane < half
    sides = []
    energy = jnp.float32(0.0)
    square = jnp.zeros((LANES, 2 * half), jnp.float32)
    for part_index in range(2):
        o = spec[:, part_index * 2 * half:(part_index + 1) * 2 * half]
        square = square + o * o
        before = jnp.where(lane == 0, 0.0, pltpu.roll(o[LANES - 16:], 1, 1))
        after = jnp.where(lane == 2 * half - 1, 0.0, pltpu.roll(o[:16], 2 * half - 1, 1))
        sides.append(
            jnp.concatenate(
                [
                    jnp.where(low16, before, o[48:64]),
                    jnp.where(low, o[:64], o[64:]),
                    jnp.where(low16, o[64:80], after),
                    jnp.zeros((32, 2 * half), jnp.float32),
                ],
                axis=0,
            ).astype(jnp.bfloat16)
        )
    energy_ref[0] = jnp.sum(square) * 0.5
    sr, si = sides
    window = jnp.concatenate(
        [jnp.concatenate([sr, si], axis=1), jnp.concatenate([-si, sr], axis=1)], axis=0
    )
    best = jnp.zeros((accels, 2 * half), jnp.float32)
    group = 8
    for g in range(LANES // 2 // group):
        out = jnp.dot(
            tmat[g * group * accels:(g + 1) * group * accels, :], window,
            preferred_element_type=jnp.float32,
        )
        for kk in range(group):
            rr = out[kk * accels:(kk + 1) * accels, :2 * half]
            ii = out[kk * accels:(kk + 1) * accels, 2 * half:]
            best = jnp.maximum(best, rr * rr + ii * ii)
    best = jnp.maximum(best, pltpu.roll(best, half, 1))
    peaks_ref[0] = best[:, :half]


def solution(mesh):
    fft, chan = mesh.shape["fft"], mesh.shape["chan"]
    cores = 2
    xs = chan // cores

    def body(filterbank, delays, template_bank, accel_index):
        channels, samples = filterbank.shape
        dms = delays.shape[1]
        accels = accel_index.shape[0]
        length = samples * fft
        blocks = samples // LANES
        span = blocks + MAXD
        wide = length // LANES
        chunk = 512
        one, twist, two = tables(length, channels * chan)
        f32, bf16 = jnp.float32, jnp.bfloat16
        vmem = pl.BlockSpec(memory_space=pltpu.VMEM)
        dma = pltpu.SemaphoreType.DMA
        return pl.pallas_call(
            functools.partial(kernel, (fft, xs, cores, dms, blocks, chunk)),
            out_shape=(
                jax.ShapeDtypeStruct((1, accels, wide // 2), f32),
                jax.ShapeDtypeStruct((1,), f32),
            ),
            in_specs=[pl.BlockSpec(memory_space=pl.ANY)] + [vmem] * 6,
            out_specs=(vmem, pl.BlockSpec(memory_space=pltpu.SMEM)),
            scratch_shapes=[
                pltpu.VMEM((samples // chunk, channels, chunk), bf16),
                pltpu.VMEM((MAXD * dms, channels), bf16),
                pltpu.VMEM((span * dms, LANES), f32),
                pltpu.VMEM((cores, xs, fft, span, LANES), f32),
                pltpu.VMEM((xs, fft, span, LANES), f32),
                pltpu.VMEM((xs, fft, span, LANES), f32),
                pltpu.VMEM((xs, fft, span, LANES), f32),
                pltpu.VMEM((fft, span, LANES), f32),
                pltpu.VMEM((fft, span, LANES), f32),
                pltpu.VMEM((wide, LANES), f32),
                pltpu.VMEM((LANES // 2 * accels, 2 * LANES), bf16),
                dma((samples // chunk,)),
                dma((xs, fft)), dma((xs, fft)),
                dma((xs, fft)), dma((xs, fft)),
                dma((fft,)), dma((fft,)),
            ],
            compiler_params=pltpu.CompilerParams(
                collective_id=0, has_side_effects=True, vmem_limit_bytes=56 * 2 ** 20
            ),
            name="search",
        )(
            filterbank, delays.T, template_bank, accel_index[None, :], one, twist, two
        )

    in_specs = (P(("beam", "chan"), "fft"), P("chan", None), P(), P())
    out_specs = (P(("beam", "fft", "chan"), None, None), P(("beam", "fft", "chan")))
    return jax.shard_map(body, mesh=mesh, in_specs=in_specs, out_specs=out_specs, check_vma=False)
```

```python
import functools

import jax
import jax.numpy as jnp
import numpy as np
from jax import lax
from jax.experimental import pallas as pl
from jax.experimental.pallas import tpu as pltpu
from jax.sharding import PartitionSpec as P

MAXD = 16
LANES = 128
MESH = pl.DeviceIdType.MESH
HIGHEST = lax.Precision.HIGHEST


def tables(length, channels_total):
    wide = length // LANES
    half = wide // 2
    rows = np.arange(LANES)
    cols = np.arange(wide)
    outs = np.arange(half)
    first = 2 * np.pi * (rows[:, None] * rows[None, :] % LANES) / LANES
    one = np.concatenate([np.cos(first), -np.sin(first)], axis=0)
    turn = 2 * np.pi * (rows[:, None] * cols[None, :] % length) / length
    scale = channels_total ** -0.5 * length ** -0.5
    twist = np.stack([np.cos(turn), np.sin(turn)]) * scale
    second = 2 * np.pi * (cols[:, None] * outs[None, :] % wide) / wide
    c2, s2 = np.cos(second), np.sin(second)
    real = np.concatenate([c2, s2], axis=0)
    imag = np.concatenate([-s2, c2], axis=0)
    two = np.concatenate([real, real, imag, imag], axis=1)
    return [jnp.asarray(t, jnp.float32) for t in (one, twist, two)]


def collect(
    sizes,
    fb_ref, delay_hbm,
    grid_ref,
    delay_ref, xbuf, picked, acc, part, r1, q, r2, total, r3,
    lsem, fsem, s1, v1, s2, v2, s3, v3,
):
    fft, xs, cores, dms, blocks, chunk = sizes
    chan = xs * cores
    span = blocks + MAXD
    f = lax.axis_index("fft")
    c = lax.axis_index("chan")
    x, core = c // cores, c % cores
    columns = fb_ref.shape[1]
    chunks = columns // chunk

    def fetch(i):
        start = pl.multiple_of(i * chunk, chunk)
        return pltpu.make_async_copy(
            fb_ref.at[:, pl.ds(start, chunk)], xbuf.at[i], fsem.at[i]
        )

    lags = pltpu.make_async_copy(delay_hbm, delay_ref, lsem)
    lags.start()
    for i in range(chunks):
        fetch(i).start()

    barrier = pltpu.get_barrier_semaphore()
    for k in range(1, cores):
        pl.semaphore_signal(
            barrier, inc=1, device_id={"chan": x * cores + (core + k) % cores}, device_id_type=MESH
        )
    for k in range(1, xs):
        pl.semaphore_signal(
            barrier, inc=1, device_id={"chan": ((x + k) % xs) * cores + core}, device_id_type=MESH
        )
    for k in range(1, fft):
        pl.semaphore_signal(barrier, inc=1, device_id={"fft": (f + k) % fft}, device_id_type=MESH)

    lags.wait()
    lag = delay_ref[...]
    for o in range(MAXD):
        picked[(MAXD - 1 - o) * dms:(MAXD - o) * dms, :] = jnp.where(lag == o, 1.0, 0.0).astype(
            jnp.bfloat16
        )
    acc[...] = jnp.zeros_like(acc)

    def gather_columns(i, carry):
        fetch(i).wait()
        for b in range(chunk // 256):
            y = jnp.dot(
                picked[...], xbuf[i, :, b * 256:(b + 1) * 256], preferred_element_type=jnp.float32
            )
            for h in range(2):
                row = pl.multiple_of((i * (chunk // LANES) + 2 * b + h + 1) * dms, dms)
                acc[pl.ds(row, MAXD * dms), :] += y[:, h * LANES:(h + 1) * LANES]
        return carry

    lax.fori_loop(0, chunks, gather_columns, 0)

    for k in range(cores):
        for s in range(xs):
            for g in range(fft):
                d = g * chan + s * cores + k
                part[k, s, g] = acc[pl.ds(d, span, stride=dms), :]

    others = (cores - 1) + (xs - 1) + (fft - 1)
    pl.semaphore_wait(barrier, others)

    peer = (core + 1) % cores
    order = list(range(1, fft)) + [0]

    def to_core(s, k):
        xd, g = (x + s) % xs, (f + k) % fft
        return pltpu.make_async_remote_copy(
            part.at[peer, xd, g], r1.at[s, k], s1.at[s, k], v1.at[s, k],
            device_id={"chan": x * cores + peer}, device_id_type=MESH,
        )

    def to_x(s, k):
        return pltpu.make_async_remote_copy(
            q.at[s, k], r2.at[s, k], s2.at[s, k], v2.at[s, k],
            device_id={"chan": ((x + s) % xs) * cores + core}, device_id_type=MESH,
        )

    def to_fft(k):
        return pltpu.make_async_remote_copy(
            total.at[k], r3.at[k], s3.at[k], v3.at[k],
            device_id={"fft": (f + k) % fft}, device_id_type=MESH,
        )

    for k in order:
        for s in list(range(1, xs)) + [0]:
            to_core(s, k).start()
    for k in order:
        for s in range(1, xs):
            to_core(s, k).wait()
            q[s, k] = part[core, (x + s) % xs, (f + k) % fft] + r1[s, k]
            to_x(s, k).start()
    for k in order:
        to_core(0, k).wait()
        value = part[core, x, (f + k) % fft] + r1[0, k]
        for s in range(1, xs):
            to_x(s, k).wait()
            value = value + r2[s, k]
        total[k] = value
        if k:
            to_fft(k).start()

    for k in range(1, fft):
        to_fft(k).wait()
    r3[0] = total[0]
    for z in range(fft):
        own = (f - z + fft) % fft
        grid_ref[z * blocks:(z + 1) * blocks, :] = r3[own, MAXD:, :]
        if z:
            grid_ref[z * blocks - MAXD:z * blocks, :] += r3[own, :MAXD, :]


def search(
    grid_hbm, bank_ref, accel_ref, one_ref, twist_ref, two_ref, peaks_ref, energy_ref,
    grid_ref, tmat, gsem,
):
    load = pltpu.make_async_copy(grid_hbm, grid_ref, gsem)
    load.start()
    accel = accel_ref[...]
    bank = bank_ref.shape[2]
    accels = accel.shape[1]
    taps = bank_ref.shape[1]
    chosen = jnp.where(
        lax.broadcasted_iota(jnp.int32, (bank, accels), 0) == accel, 1.0, 0.0
    ).astype(jnp.bfloat16)
    rows = []
    for part_index in range(2):
        row = jnp.dot(bank_ref[part_index], chosen, preferred_element_type=jnp.float32)
        row = jnp.concatenate([row, jnp.zeros((LANES - taps, accels), jnp.float32)], axis=0)
        rows.append(row.T)
    for kk in range(LANES // 2):
        for part_index in range(2):
            shifted = pltpu.roll(rows[part_index], kk, 1) if kk else rows[part_index]
            tmat[kk * accels:(kk + 1) * accels, part_index * LANES:(part_index + 1) * LANES] = (
                shifted.astype(jnp.bfloat16)
            )

    load.wait()
    wide = grid_ref.shape[0]
    half = wide // 2
    data = grid_ref[...] if wide == LANES else grid_ref[...].reshape(LANES, wide)
    mixed = jnp.dot(one_ref[...], data, precision=HIGHEST, preferred_element_type=jnp.float32)
    re, im = mixed[:LANES], mixed[LANES:]
    tc, ts = twist_ref[0], twist_ref[1]
    turned = jnp.concatenate([re * tc + im * ts, im * tc - re * ts], axis=1)
    spec = jnp.dot(turned, two_ref[...], precision=HIGHEST, preferred_element_type=jnp.float32)

    lane = lax.broadcasted_iota(jnp.int32, (16, 2 * half), 1)
    low = lax.broadcasted_iota(jnp.int32, (64, 2 * half), 1) < half
    low16 = lane < half
    sides = []
    energy = jnp.float32(0.0)
    square = jnp.zeros((LANES, 2 * half), jnp.float32)
    for part_index in range(2):
        o = spec[:, part_index * 2 * half:(part_index + 1) * 2 * half]
        square = square + o * o
        before = jnp.where(lane == 0, 0.0, pltpu.roll(o[LANES - 16:], 1, 1))
        after = jnp.where(lane == 2 * half - 1, 0.0, pltpu.roll(o[:16], 2 * half - 1, 1))
        sides.append(
            jnp.concatenate(
                [
                    jnp.where(low16, before, o[48:64]),
                    jnp.where(low, o[:64], o[64:]),
                    jnp.where(low16, o[64:80], after),
                    jnp.zeros((32, 2 * half), jnp.float32),
                ],
                axis=0,
            ).astype(jnp.bfloat16)
        )
    energy_ref[0] = jnp.sum(square) * 0.5
    sr, si = sides
    window = jnp.concatenate(
        [jnp.concatenate([sr, si], axis=1), jnp.concatenate([-si, sr], axis=1)], axis=0
    )
    best = jnp.zeros((accels, 2 * half), jnp.float32)
    group = 8
    for g in range(LANES // 2 // group):
        out = jnp.dot(
            tmat[g * group * accels:(g + 1) * group * accels, :], window,
            preferred_element_type=jnp.float32,
        )
        for kk in range(group):
            rr = out[kk * accels:(kk + 1) * accels, :2 * half]
            ii = out[kk * accels:(kk + 1) * accels, 2 * half:]
            best = jnp.maximum(best, rr * rr + ii * ii)
    best = jnp.maximum(best, pltpu.roll(best, half, 1))
    peaks_ref[0] = best[:, :half]


def solution(mesh):
    fft, chan = mesh.shape["fft"], mesh.shape["chan"]
    cores = 2
    xs = chan // cores

    def body(filterbank, delays, template_bank, accel_index):
        channels, samples = filterbank.shape
        dms = delays.shape[1]
        accels = accel_index.shape[0]
        length = samples * fft
        blocks = samples // LANES
        span = blocks + MAXD
        wide = length // LANES
        chunk = 512
        one, twist, two = tables(length, channels * chan)
        f32, bf16 = jnp.float32, jnp.bfloat16
        vmem = pl.BlockSpec(memory_space=pltpu.VMEM)
        dma = pltpu.SemaphoreType.DMA
        hbm = pl.BlockSpec(memory_space=pltpu.HBM)
        grid = pl.pallas_call(
            functools.partial(collect, (fft, xs, cores, dms, blocks, chunk)),
            out_shape=jax.ShapeDtypeStruct((wide, LANES), f32),
            in_specs=[hbm] * 2,
            out_specs=vmem,
            scratch_shapes=[
                pltpu.VMEM((dms, channels), jnp.int32),
                pltpu.VMEM((samples // chunk, channels, chunk), bf16),
                pltpu.VMEM((MAXD * dms, channels), bf16),
                pltpu.VMEM((span * dms, LANES), f32),
                pltpu.VMEM((cores, xs, fft, span, LANES), f32),
                pltpu.VMEM((xs, fft, span, LANES), f32),
                pltpu.VMEM((xs, fft, span, LANES), f32),
                pltpu.VMEM((xs, fft, span, LANES), f32),
                pltpu.VMEM((fft, span, LANES), f32),
                pltpu.VMEM((fft, span, LANES), f32),
                dma,
                dma((samples // chunk,)),
                dma((xs, fft)), dma((xs, fft)),
                dma((xs, fft)), dma((xs, fft)),
                dma((fft,)), dma((fft,)),
            ],
            compiler_params=pltpu.CompilerParams(
                collective_id=0, has_side_effects=True, vmem_limit_bytes=56 * 2 ** 20
            ),
            name="collect",
        )(filterbank, delays.T)
        return pl.pallas_call(
            search,
            out_shape=(
                jax.ShapeDtypeStruct((1, accels, wide // 2), f32),
                jax.ShapeDtypeStruct((1,), f32),
            ),
            in_specs=[hbm] + [vmem] * 5,
            out_specs=(vmem, pl.BlockSpec(memory_space=pltpu.SMEM)),
            scratch_shapes=[
                pltpu.VMEM((wide, LANES), f32),
                pltpu.VMEM((LANES // 2 * accels, 2 * LANES), bf16),
                dma,
            ],
            compiler_params=pltpu.CompilerParams(vmem_limit_bytes=24 * 2 ** 20),
            name="search",
        )(grid, template_bank.transpose(0, 2, 1), accel_index[None, :], one, twist, two)

    in_specs = (P(("beam", "chan"), "fft"), P("chan", None), P(), P())
    out_specs = (P(("beam", "fft", "chan"), None, None), P(("beam", "fft", "chan")))
    return jax.shard_map(body, mesh=mesh, in_specs=in_specs, out_specs=out_specs, check_vma=False)
```

```python
import functools

import jax
import jax.numpy as jnp
import numpy as np
from jax import lax
from jax.experimental import pallas as pl
from jax.experimental.pallas import tpu as pltpu
from jax.sharding import PartitionSpec as P

MAXD = 16
LANES = 128
MESH = pl.DeviceIdType.MESH
HIGHEST = lax.Precision.HIGHEST


def tables(length, channels_total):
    wide = length // LANES
    half = wide // 2
    rows = np.arange(LANES)
    cols = np.arange(wide)
    outs = np.arange(half)
    first = 2 * np.pi * (rows[:, None] * rows[None, :] % LANES) / LANES
    one = np.concatenate([np.cos(first), -np.sin(first)], axis=0)
    turn = 2 * np.pi * (rows[:, None] * cols[None, :] % length) / length
    scale = channels_total ** -0.5 * length ** -0.5
    twist = np.stack([np.cos(turn), np.sin(turn)]) * scale
    second = 2 * np.pi * (cols[:, None] * outs[None, :] % wide) / wide
    c2, s2 = np.cos(second), np.sin(second)
    real = np.concatenate([c2, s2], axis=0)
    imag = np.concatenate([-s2, c2], axis=0)
    two = np.concatenate([real, real, imag, imag], axis=1)
    return [jnp.asarray(t, jnp.float32) for t in (one, twist, two)]


def collect(
    sizes,
    fb_ref, delay_hbm,
    grid_ref,
    delay_ref, xbuf, picked, acc, part, r1, q, r2, total, r3,
    lsem, fsem, s1, v1, s2, v2, s3, v3,
):
    fft, xs, cores, dms, blocks, chunk = sizes
    chan = xs * cores
    span = blocks + MAXD
    f = lax.axis_index("fft")
    c = lax.axis_index("chan")
    x, core = c // cores, c % cores
    columns = fb_ref.shape[1]
    chunks = columns // chunk

    def fetch(i):
        start = pl.multiple_of(i * chunk, chunk)
        return pltpu.make_async_copy(
            fb_ref.at[:, pl.ds(start, chunk)], xbuf.at[i], fsem.at[i]
        )

    lags = pltpu.make_async_copy(delay_hbm, delay_ref, lsem)
    lags.start()
    ahead = min(2, chunks)
    for i in range(ahead):
        fetch(i).start()

    barrier = pltpu.get_barrier_semaphore()
    for k in range(1, cores):
        pl.semaphore_signal(
            barrier, inc=1, device_id={"chan": x * cores + (core + k) % cores}, device_id_type=MESH
        )
    for k in range(1, xs):
        pl.semaphore_signal(
            barrier, inc=1, device_id={"chan": ((x + k) % xs) * cores + core}, device_id_type=MESH
        )
    for k in range(1, fft):
        pl.semaphore_signal(barrier, inc=1, device_id={"fft": (f + k) % fft}, device_id_type=MESH)

    lags.wait()
    lag = delay_ref[...]
    for o in range(MAXD):
        picked[(MAXD - 1 - o) * dms:(MAXD - o) * dms, :] = jnp.where(lag == o, 1.0, 0.0).astype(
            jnp.bfloat16
        )
    acc[...] = jnp.zeros_like(acc)

    def gather_columns(i, carry):
        fetch(i).wait()

        @pl.when(i + ahead < chunks)
        def _():
            fetch(i + ahead).start()

        for b in range(chunk // 256):
            y = jnp.dot(
                picked[...], xbuf[i, :, b * 256:(b + 1) * 256], preferred_element_type=jnp.float32
            )
            for h in range(2):
                row = pl.multiple_of((i * (chunk // LANES) + 2 * b + h + 1) * dms, dms)
                acc[pl.ds(row, MAXD * dms), :] += y[:, h * LANES:(h + 1) * LANES]
        return carry

    lax.fori_loop(0, chunks, gather_columns, 0)

    for k in range(cores):
        for s in range(xs):
            for g in range(fft):
                d = g * chan + s * cores + k
                part[k, s, g] = acc[pl.ds(d, span, stride=dms), :]

    others = (cores - 1) + (xs - 1) + (fft - 1)
    pl.semaphore_wait(barrier, others)

    peer = (core + 1) % cores
    order = list(range(1, fft)) + [0]

    def to_core(s, k):
        xd, g = (x + s) % xs, (f + k) % fft
        return pltpu.make_async_remote_copy(
            part.at[peer, xd, g], r1.at[s, k], s1.at[s, k], v1.at[s, k],
            device_id={"chan": x * cores + peer}, device_id_type=MESH,
        )

    def to_x(s, k):
        return pltpu.make_async_remote_copy(
            q.at[s, k], r2.at[s, k], s2.at[s, k], v2.at[s, k],
            device_id={"chan": ((x + s) % xs) * cores + core}, device_id_type=MESH,
        )

    def to_fft(k):
        return pltpu.make_async_remote_copy(
            total.at[k], r3.at[k], s3.at[k], v3.at[k],
            device_id={"fft": (f + k) % fft}, device_id_type=MESH,
        )

    for k in order:
        for s in list(range(1, xs)) + [0]:
            to_core(s, k).start()
    for k in order:
        for s in range(1, xs):
            to_core(s, k).wait()
            q[s, k] = part[core, (x + s) % xs, (f + k) % fft] + r1[s, k]
            to_x(s, k).start()
    for k in order:
        to_core(0, k).wait()
        value = part[core, x, (f + k) % fft] + r1[0, k]
        for s in range(1, xs):
            to_x(s, k).wait()
            value = value + r2[s, k]
        total[k] = value
        if k:
            to_fft(k).start()

    for k in range(1, fft):
        to_fft(k).wait()
    r3[0] = total[0]
    for z in range(fft):
        own = (f - z + fft) % fft
        grid_ref[z * blocks:(z + 1) * blocks, :] = r3[own, MAXD:, :]
        if z:
            grid_ref[z * blocks - MAXD:z * blocks, :] += r3[own, :MAXD, :]


def search(
    grid_hbm, bank_ref, accel_ref, one_ref, twist_ref, two_ref, peaks_ref, energy_ref,
    grid_ref, tmat, gsem,
):
    load = pltpu.make_async_copy(grid_hbm, grid_ref, gsem)
    load.start()
    accel = accel_ref[...]
    bank = bank_ref.shape[2]
    accels = accel.shape[1]
    taps = bank_ref.shape[1]
    chosen = jnp.where(
        lax.broadcasted_iota(jnp.int32, (bank, accels), 0) == accel, 1.0, 0.0
    ).astype(jnp.bfloat16)
    rows = []
    for part_index in range(2):
        row = jnp.dot(bank_ref[part_index], chosen, preferred_element_type=jnp.float32)
        row = jnp.concatenate([row, jnp.zeros((LANES - taps, accels), jnp.float32)], axis=0)
        rows.append(row.T)
    for kk in range(LANES // 2):
        for part_index in range(2):
            shifted = pltpu.roll(rows[part_index], kk, 1) if kk else rows[part_index]
            tmat[kk * accels:(kk + 1) * accels, part_index * LANES:(part_index + 1) * LANES] = (
                shifted.astype(jnp.bfloat16)
            )

    load.wait()
    wide = grid_ref.shape[0]
    half = wide // 2
    data = grid_ref[...] if wide == LANES else grid_ref[...].reshape(LANES, wide)
    mixed = jnp.dot(one_ref[...], data, precision=HIGHEST, preferred_element_type=jnp.float32)
    re, im = mixed[:LANES], mixed[LANES:]
    tc, ts = twist_ref[0], twist_ref[1]
    turned = jnp.concatenate([re * tc + im * ts, im * tc - re * ts], axis=1)
    spec = jnp.dot(turned, two_ref[...], precision=HIGHEST, preferred_element_type=jnp.float32)

    lane = lax.broadcasted_iota(jnp.int32, (16, 2 * half), 1)
    low = lax.broadcasted_iota(jnp.int32, (64, 2 * half), 1) < half
    low16 = lane < half
    sides = []
    energy = jnp.float32(0.0)
    square = jnp.zeros((LANES, 2 * half), jnp.float32)
    for part_index in range(2):
        o = spec[:, part_index * 2 * half:(part_index + 1) * 2 * half]
        square = square + o * o
        before = jnp.where(lane == 0, 0.0, pltpu.roll(o[LANES - 16:], 1, 1))
        after = jnp.where(lane == 2 * half - 1, 0.0, pltpu.roll(o[:16], 2 * half - 1, 1))
        sides.append(
            jnp.concatenate(
                [
                    jnp.where(low16, before, o[48:64]),
                    jnp.where(low, o[:64], o[64:]),
                    jnp.where(low16, o[64:80], after),
                    jnp.zeros((32, 2 * half), jnp.float32),
                ],
                axis=0,
            ).astype(jnp.bfloat16)
        )
    energy_ref[0] = jnp.sum(square) * 0.5
    sr, si = sides
    window = jnp.concatenate(
        [jnp.concatenate([sr, si], axis=1), jnp.concatenate([-si, sr], axis=1)], axis=0
    )
    best = jnp.zeros((accels, 2 * half), jnp.float32)
    group = 8
    for g in range(LANES // 2 // group):
        out = jnp.dot(
            tmat[g * group * accels:(g + 1) * group * accels, :], window,
            preferred_element_type=jnp.float32,
        )
        for kk in range(group):
            rr = out[kk * accels:(kk + 1) * accels, :2 * half]
            ii = out[kk * accels:(kk + 1) * accels, 2 * half:]
            best = jnp.maximum(best, rr * rr + ii * ii)
    best = jnp.maximum(best, pltpu.roll(best, half, 1))
    peaks_ref[0] = best[:, :half]


def solution(mesh):
    fft, chan = mesh.shape["fft"], mesh.shape["chan"]
    cores = 2
    xs = chan // cores

    def body(filterbank, delays, template_bank, accel_index):
        channels, samples = filterbank.shape
        dms = delays.shape[1]
        accels = accel_index.shape[0]
        length = samples * fft
        blocks = samples // LANES
        span = blocks + MAXD
        wide = length // LANES
        chunk = 1024
        one, twist, two = tables(length, channels * chan)
        f32, bf16 = jnp.float32, jnp.bfloat16
        vmem = pl.BlockSpec(memory_space=pltpu.VMEM)
        dma = pltpu.SemaphoreType.DMA
        hbm = pl.BlockSpec(memory_space=pltpu.HBM)
        grid = pl.pallas_call(
            functools.partial(collect, (fft, xs, cores, dms, blocks, chunk)),
            out_shape=jax.ShapeDtypeStruct((wide, LANES), f32),
            in_specs=[hbm] * 2,
            out_specs=vmem,
            scratch_shapes=[
                pltpu.VMEM((dms, channels), jnp.int32),
                pltpu.VMEM((samples // chunk, channels, chunk), bf16),
                pltpu.VMEM((MAXD * dms, channels), bf16),
                pltpu.VMEM((span * dms, LANES), f32),
                pltpu.VMEM((cores, xs, fft, span, LANES), f32),
                pltpu.VMEM((xs, fft, span, LANES), f32),
                pltpu.VMEM((xs, fft, span, LANES), f32),
                pltpu.VMEM((xs, fft, span, LANES), f32),
                pltpu.VMEM((fft, span, LANES), f32),
                pltpu.VMEM((fft, span, LANES), f32),
                dma,
                dma((samples // chunk,)),
                dma((xs, fft)), dma((xs, fft)),
                dma((xs, fft)), dma((xs, fft)),
                dma((fft,)), dma((fft,)),
            ],
            compiler_params=pltpu.CompilerParams(
                collective_id=0, has_side_effects=True, vmem_limit_bytes=56 * 2 ** 20
            ),
            name="collect",
        )(filterbank, delays.T)
        return pl.pallas_call(
            search,
            out_shape=(
                jax.ShapeDtypeStruct((1, accels, wide // 2), f32),
                jax.ShapeDtypeStruct((1,), f32),
            ),
            in_specs=[hbm] + [vmem] * 5,
            out_specs=(vmem, pl.BlockSpec(memory_space=pltpu.SMEM)),
            scratch_shapes=[
                pltpu.VMEM((wide, LANES), f32),
                pltpu.VMEM((LANES // 2 * accels, 2 * LANES), bf16),
                dma,
            ],
            compiler_params=pltpu.CompilerParams(vmem_limit_bytes=24 * 2 ** 20),
            name="search",
        )(grid, template_bank.transpose(0, 2, 1), accel_index[None, :], one, twist, two)

    in_specs = (P(("beam", "chan"), "fft"), P("chan", None), P(), P())
    out_specs = (P(("beam", "fft", "chan"), None, None), P(("beam", "fft", "chan")))
    return jax.shard_map(body, mesh=mesh, in_specs=in_specs, out_specs=out_specs, check_vma=False)
```
